512 devices in a mesh: grp: 4 (over x), gx: 16 (over z, y_hi), gy: 8 (over y_lo, core).
Axes of the slice: x: 4, y: 8 (y_hi: 2, y_lo: 4; y = y_hi * 4 + y_lo), z: 8, core: 2. Of those that a mesh axis runs over, the one named last changes fastest.
Arguments:
- solid_velocity: float32 [3, 16, 256, 4096], P(None, 'grp', 'gx', 'gy'), may hold values from -6 to 6
- solid_stress: float32 [6, 16, 256, 4096], P(None, 'grp', 'gx', 'gy'), may hold values from -6 to 6
- ocean_pressure: float32 [8, 256, 4096], P(None, 'gx', ('grp', 'gy')), may hold values from -6 to 6
- ocean_velocity: float32 [3, 8, 256, 4096], P(None, None, 'gx', ('grp', 'gy')), may hold values from -4 to 4
- surface: float32 [256, 4096], P('gx', ('grp', 'gy')), may hold values from -6 to 6
- materials: float32 [3, 8], replicated, may hold values from 0.5 to 1.5
- region_ids: int32 [16, 256, 4096], P('grp', 'gx', 'gy'), may hold values from 0 to 7
- fault_mask: int32 [16, 256, 4096], P('grp', 'gx', 'gy'), may hold values 0 or 1
- plastic_params: float32 [2], replicated, may hold values from 0.3 to 0.6
Outputs:
- velocity_out: float32 [3, 16, 256, 4096], P(None, 'grp', 'gx', 'gy')
- stress_out: float32 [6, 16, 256, 4096], P(None, 'grp', 'gx', 'gy')
- pressure_out: float32 [8, 256, 4096], P(None, 'gx', ('grp', 'gy'))
- flow_out: float32 [3, 8, 256, 4096], P(None, None, 'gx', ('grp', 'gy'))
- surface_out: float32 [256, 4096], P('gx', ('grp', 'gy'))
The draws below stay inside these ranges and needn't reach their ends.
All inputs are finite; a program needn't handle non-finite values. No bound on the sum of `fault_mask` on one device may be relied on, other than what follows from the above.
Results may differ from the reference program's by a relative error of at most 0.00002.
Values sent between devices are 32-bit elements; how exact they have to be, the bound alone decides.
A program may use at most 64 MiB of HBM per device.

```python
import jax
import jax.numpy as jnp
from jax import lax

OZ = 8
STEPS = 2
REGIONS = 8
NZ = 16
NX = 256
NY = 4096


def place_ends(array, key, smallest, largest):
    longest = array.shape.index(max(array.shape))
    spots = []
    for shift in (0, 1):
        where = [jax.random.randint(jax.random.fold_in(key, axis), (), 0, length) for axis, length in enumerate(array.shape)]
        where[longest] = (where[longest] + shift) % array.shape[longest]
        spots.append(tuple(where))
    return array.at[spots[0]].set(smallest).at[spots[1]].set(largest)


def level_of(key, dims, split, smallest, high):
    def one(axis_at, blocks):
        draws = jax.random.uniform(jax.random.fold_in(jax.random.fold_in(key, 6), axis_at), (blocks,), jnp.float32, smallest / len(split), high / len(split))
        return jnp.repeat(jnp.exp(draws), dims[axis_at] // blocks).reshape((-1,) + (1,) * (len(dims) - axis_at - 1))

    loudness = one(*split[0])
    for cut in split[1:]:
        loudness = loudness * one(*cut)
    return loudness


def centred(key, dims, width, limit, shards=(), dtype=jnp.bfloat16):
    gain = level_of(key, dims, shards, -0.22, 0.18) if shards else 1.0
    array = jax.random.normal(key, dims, jnp.float32) * width * gain
    return jnp.minimum(jnp.maximum(array, -limit), limit).astype(dtype)


def setup_inputs(seed: int = 0) -> dict:
    seeds = jax.random.split(jax.random.key(seed), 10)
    return {
        "solid_velocity": centred(seeds[0], (3, NZ, NX, NY), 1.0, 6.0, ((1, 4), (2, 16), (3, 8)), jnp.float32),
        "solid_stress": centred(seeds[1], (6, NZ, NX, NY), 1.0, 6.0, ((1, 4), (2, 16), (3, 8)), jnp.float32),
        "ocean_pressure": centred(seeds[2], (OZ, NX, NY), 1.0, 6.0, ((1, 16), (2, 32)), jnp.float32),
        "ocean_velocity": centred(seeds[3], (3, OZ, NX, NY), 0.5, 4.0, ((2, 16), (3, 32)), jnp.float32),
        "surface": centred(seeds[4], (NX, NY), 1.0, 6.0, ((0, 16), (1, 32)), jnp.float32),
        "materials": jnp.clip(jax.random.uniform(seeds[5], (3, REGIONS), jnp.float32, 0.5, 1.5), 0.5, 1.5),
        "region_ids": place_ends(jax.random.randint(seeds[6], (NZ, NX, NY), 0, REGIONS), jax.random.fold_in(seeds[6], 1), 0, REGIONS - 1).astype(jnp.int32),
        "fault_mask": place_ends((jax.random.randint(seeds[7], (NZ, NX, NY), 0, 3) < 1).astype(jnp.int32), jax.random.fold_in(seeds[7], 1), 0, 1),
        "plastic_params": jnp.clip(jax.random.uniform(seeds[8], (2,), jnp.float32, 0.3, 0.6), 0.3, 0.6),
    }


courant_number = 0.2
ocean_step = 0.3
vertical_step = 0.3
gravity_term = 0.5
surface_step = 0.3

def before(field, axis):
    widths = [(0, 0)] * field.ndim
    widths[axis] = (1, 0)
    return lax.slice_in_dim(jnp.pad(field, widths), 0, field.shape[axis], axis=axis)

def after(field, axis):
    widths = [(0, 0)] * field.ndim
    widths[axis] = (0, 1)
    return lax.slice_in_dim(jnp.pad(field, widths), 1, field.shape[axis] + 1, axis=axis)

def lookup(region_ids, row_values):
    total = jnp.zeros(region_ids.shape, jnp.float32)
    for region in range(REGIONS):
        total = total + jnp.where(region_ids == region, row_values[region], jnp.zeros((), jnp.float32))
    return total

def yield_cap(stress_xx_part, stress_yy_part, stress_zz_part, sxy, sxz, syz, fault_mask, plastic_params):
    mean = (stress_xx_part + stress_yy_part + stress_zz_part) / 3.0
    dxx, dyy, dzz = (stress_xx_part - mean, stress_yy_part - mean, stress_zz_part - mean)
    tau = jnp.sqrt(0.5 * (dxx * dxx + dyy * dyy + dzz * dzz) + sxy * sxy + sxz * sxz + syz * syz)
    strength = plastic_params[0] + plastic_params[1] * jnp.maximum(-mean, 0.0)
    factor = strength / jnp.maximum(tau, strength)
    factor = jnp.where(fault_mask == 1, factor, jnp.ones((), jnp.float32))
    return (mean + dxx * factor, mean + dyy * factor, mean + dzz * factor, sxy * factor, sxz * factor, syz * factor)

def reference(solid_velocity, solid_stress, ocean_pressure, ocean_velocity, surface, materials, region_ids, fault_mask, plastic_params):
    lame_lambda = lookup(region_ids, materials[0])
    shear_modulus = lookup(region_ids, materials[1])
    buoy = lookup(region_ids, materials[2])
    vx, vy, vz = (solid_velocity[0], solid_velocity[1], solid_velocity[2])
    stress_xx_part, stress_yy_part, stress_zz_part, sxy, sxz, syz = [solid_stress[k] for k in range(6)]
    press = ocean_pressure
    flow_x, flow_y, lift = (ocean_velocity[0], ocean_velocity[1], ocean_velocity[2])
    height = surface
    for step in range(STEPS):
        szz_above = jnp.concatenate([-press[0][None], stress_zz_part[:-1]], axis=0)
        div_x = stress_xx_part - before(stress_xx_part, 1) + (sxy - before(sxy, 2)) + (sxz - before(sxz, 0))
        div_y = sxy - before(sxy, 1) + (stress_yy_part - before(stress_yy_part, 2)) + (syz - before(syz, 0))
        div_z = sxz - before(sxz, 1) + (syz - before(syz, 2)) + (stress_zz_part - szz_above)
        vx = vx + courant_number * buoy * div_x
        vy = vy + courant_number * buoy * div_y
        vz = vz + courant_number * buoy * div_z
        gradient_xx_part, gxy, gxz = (after(vx, 1) - vx, after(vx, 2) - vx, after(vx, 0) - vx)
        gyx, gradient_yy_part, gyz = (after(vy, 1) - vy, after(vy, 2) - vy, after(vy, 0) - vy)
        gzx, gzy, gradient_zz_part = (after(vz, 1) - vz, after(vz, 2) - vz, after(vz, 0) - vz)
        dilatation = gradient_xx_part + gradient_yy_part + gradient_zz_part
        stress_xx_part = stress_xx_part + courant_number * (lame_lambda * dilatation + 2.0 * shear_modulus * gradient_xx_part)
        stress_yy_part = stress_yy_part + courant_number * (lame_lambda * dilatation + 2.0 * shear_modulus * gradient_yy_part)
        stress_zz_part = stress_zz_part + courant_number * (lame_lambda * dilatation + 2.0 * shear_modulus * gradient_zz_part)
        sxy = sxy + courant_number * shear_modulus * (gxy + gyx)
        sxz = sxz + courant_number * shear_modulus * (gxz + gzx)
        syz = syz + courant_number * shear_modulus * (gyz + gzy)
        stress_xx_part, stress_yy_part, stress_zz_part, sxy, sxz, syz = yield_cap(stress_xx_part, stress_yy_part, stress_zz_part, sxy, sxz, syz, fault_mask, plastic_params)
        flow_x = flow_x - ocean_step * (after(press, 1) - press)
        flow_y = flow_y - ocean_step * (after(press, 2) - press)
        above = jnp.concatenate([press[1:], (gravity_term * height)[None]], axis=0)
        lift = lift - vertical_step * (above - press)
        lift_below = jnp.concatenate([vz[0][None], lift[:-1]], axis=0)
        press = press - ocean_step * (flow_x - before(flow_x, 1) + (flow_y - before(flow_y, 2))) - vertical_step * (lift - lift_below)
        height = height + surface_step * lift[-1]
    return (jnp.stack([vx, vy, vz]), jnp.stack([stress_xx_part, stress_yy_part, stress_zz_part, sxy, sxz, syz]), press, jnp.stack([flow_x, flow_y, lift]), height)
```

```python
import functools

import jax
import jax.numpy as jnp
from jax import lax
from jax.experimental import pallas as pl
from jax.experimental.pallas import tpu as pltpu
from jax.sharding import PartitionSpec as P

STEPS = 2
REGIONS = 8

courant_number = 0.2
ocean_step = 0.3
vertical_step = 0.3
gravity_term = 0.5
surface_step = 0.3

MESH = pl.DeviceIdType.MESH
F32 = jnp.float32
XX, YY, ZZ, XY, XZ, YZ = range(6)
ALONG_X = (XX, XY, XZ)
ALONG_Y = (XY, YY, YZ)
ALONG_Z = (XZ, YZ, ZZ)


class Route:
    def __init__(self, src, dst, send_sem, recv_sem, device, sends, receives):
        self.copy = pltpu.make_async_remote_copy(
            src_ref=src,
            dst_ref=dst,
            send_sem=send_sem,
            recv_sem=recv_sem,
            device_id=device,
            device_id_type=MESH,
        )
        self.sends, self.receives = sends, receives

    def start(self):
        pl.when(self.sends)(self.copy.start)

    def wait_recv(self):
        pl.when(self.receives)(self.copy.wait_recv)

    def wait_send(self):
        pl.when(self.sends)(self.copy.wait_send)


def kernel(
    sizes,
    velocity_in,
    stress_in,
    pressure_in,
    flow_in,
    surface_in,
    materials_in,
    regions_in,
    fault_in,
    plastic_in,
    velocity_out,
    stress_out,
    pressure_out,
    flow_out,
    surface_out,
    S,
    V,
    PR,
    FL,
    H,
    ID,
    FM,
    LAM,
    MU,
    BU,
    xs_send,
    xs_recv,
    xv_send,
    xv_recv,
    ys_send,
    ys_recv,
    yv_send,
    yv_recv,
    zs_recv,
    zv_recv,
    YH,
    opx_send,
    opx_recv,
    oux_send,
    oux_recv,
    opy_send,
    opy_recv,
    ouy_send,
    ouy_recv,
    load_send,
    load_recv,
    floor_recv,
    mat,
    plastic,
    in_sem,
    out_sem,
    send_sem,
    recv_sem,
):
    n_grp, n_gx, n_gy = sizes
    nz, nx, ny = ID.shape
    oz, _, ow = PR.shape
    lanes = ys_send.shape[-1]
    g, a, b = lax.axis_index("grp"), lax.axis_index("gx"), lax.axis_index("gy")

    loads = [
        pltpu.make_async_copy(source, target, in_sem.at[k])
        for k, (source, target) in enumerate(
            (
                (stress_in, S.at[:, pl.ds(1, nz)]),
                (pressure_in, PR),
                (flow_in, FL),
                (materials_in, mat),
                (regions_in, ID),
                (velocity_in, V.at[:, pl.ds(0, nz)]),
                (surface_in, H),
                (fault_in, FM),
                (plastic_in, plastic),
            )
        )
    ]
    for load in loads:
        load.start()

    rank = g * n_gy + b
    n_rank = n_grp * n_gy
    xp, xn = a > 0, a < n_gx - 1
    yp, yn = b > 0, b < n_gy - 1
    zp, zn = g > 0, g < n_grp - 1
    rp, rn = rank > 0, rank < n_rank - 1
    dev_xp, dev_xn = (g, jnp.maximum(a - 1, 0), b), (g, jnp.minimum(a + 1, n_gx - 1), b)
    dev_yp, dev_yn = (g, a, jnp.maximum(b - 1, 0)), (g, a, jnp.minimum(b + 1, n_gy - 1))
    dev_zp, dev_zn = (jnp.maximum(g - 1, 0), a, b), (jnp.minimum(g + 1, n_grp - 1), a, b)

    def of_rank(r):
        return (r // n_gy, a, r % n_gy)

    dev_rp = of_rank(jnp.maximum(rank - 1, 0))
    dev_rn = of_rank(jnp.minimum(rank + 1, n_rank - 1))
    top = g == 0
    solid = rank // n_grp
    quarter = rank % n_grp
    dev_solid = (0, a, solid)
    self_solid = top & (solid == b)
    owners = [of_rank(b * n_grp + q) for q in range(n_grp)]
    self_owner = [top & (b * n_grp + q == b) for q in range(n_grp)]

    barrier = pltpu.get_barrier_semaphore()
    partners = [
        (xp, dev_xp),
        (xn, dev_xn),
        (yp, dev_yp),
        (yn, dev_yn),
        (zp, dev_zp),
        (zn, dev_zn),
        (rp, dev_rp),
        (rn, dev_rn),
        (jnp.logical_not(self_solid), dev_solid),
    ] + [(top & jnp.logical_not(self_owner[q]), owners[q]) for q in range(n_grp)]
    expected = 0
    for there, device in partners:
        expected = expected + there.astype(jnp.int32)

        @pl.when(there)
        def _(device=device):
            pl.semaphore_signal(barrier, inc=1, device_id=device, device_id_type=MESH)

    for missing, buffers in (
        (xp, (xs_recv, oux_recv)),
        (xn, (xv_recv, opx_recv)),
        (yp, (ys_recv,)),
        (yn, (yv_recv,)),
        (zp, (zs_recv,)),
        (zn, (zv_recv,)),
        (rp, (ouy_recv,)),
        (rn, (opy_recv,)),
    ):

        @pl.when(jnp.logical_not(missing))
        def _(buffers=buffers):
            for buffer in buffers:
                buffer[...] = jnp.zeros(buffer.shape, F32)

    lane = lax.broadcasted_iota(jnp.int32, (nx, lanes), 1)
    row = lax.broadcasted_iota(jnp.int32, (nx, ny), 0)
    col = lax.broadcasted_iota(jnp.int32, (nx, ny), 1)
    orow = lax.broadcasted_iota(jnp.int32, (nx, ow), 0)
    ocol = lax.broadcasted_iota(jnp.int32, (nx, ow), 1)

    def shift(tile, start, stop):
        amount = (stop - start) % tile.shape[1]
        return pltpu.roll(tile, amount, 1) if amount else tile

    def pack_rows(target, field, planes, comps, at):
        for z in range(nz):
            for k, c in enumerate(comps):
                target[z, k : k + 1, :] = field[c, z + planes, at : at + 1, :]

    def pack_cols(field, planes, comps, at):
        first = (at // lanes) * lanes
        packed = jnp.zeros((nx, lanes), F32)
        for z in range(nz):
            for k, c in enumerate(comps):
                tile = field[c, z + planes, :, first : first + lanes]
                slot = z * 3 + k
                packed = jnp.where(lane == slot, shift(tile, at - first, slot), packed)
        return packed

    def unpack_cols(packed, at):
        for z in range(nz):
            for k in range(3):
                YH[k, z] = shift(packed, z * 3 + k, at)

    def widen(tile, last):
        if ny == lanes:
            return tile
        blank = jnp.zeros((nx, ny - lanes), F32)
        return jnp.concatenate([blank, tile] if last else [tile, blank], axis=1)

    n_msg = 15

    def routes(t):
        base = t * n_msg

        def route(k, src, dst, device, sends, receives):
            return Route(src, dst, send_sem.at[base + k], recv_sem.at[base + k], device, sends, receives)

        stress = [
            route(0, xs_send.at[t], xs_recv.at[t], dev_xn, xn, xp),
            route(1, ys_send.at[t], ys_recv.at[t], dev_yn, yn, yp),
            route(2, S.at[pl.ds(XZ, 2), nz], zs_recv.at[t, pl.ds(0, 2)], dev_zn, zn, zp),
            route(3, S.at[pl.ds(ZZ, 1), nz], zs_recv.at[t, pl.ds(2, 1)], dev_zn, zn, zp),
        ]
        motion = [
            route(4, xv_send.at[t], xv_recv.at[t], dev_xp, xp, xn),
            route(5, yv_send.at[t], yv_recv.at[t], dev_yp, yp, yn),
            route(6, V.at[:, 0], zv_recv.at[t], dev_zp, zp, zn),
        ]
        ocean = [
            route(7, opx_send.at[t], opx_recv.at[t], dev_xp, xp, xn),
            route(8, oux_send.at[t], oux_recv.at[t], dev_xn, xn, xp),
            route(9, opy_send.at[t], opy_recv.at[t], dev_rp, rp, rn),
            route(10, ouy_send.at[t], ouy_recv.at[t], dev_rn, rn, rp),
        ]
        return stress, motion, ocean

    def load_copies(t):
        k = t * n_msg + 11
        far = pltpu.make_async_remote_copy(
            src_ref=load_send.at[t],
            dst_ref=load_recv.at[t, quarter],
            send_sem=send_sem.at[k],
            recv_sem=recv_sem.at[k + quarter],
            device_id=dev_solid,
            device_id_type=MESH,
        )
        near = pltpu.make_async_copy(load_send.at[t], load_recv.at[t, quarter], recv_sem.at[k + quarter])
        return far, near

    def send_load(t):
        far, near = load_copies(t)
        pl.when(jnp.logical_not(self_solid))(far.start)
        pl.when(self_solid)(near.start)

    def wait_load_sent(t):
        far, _ = load_copies(t)
        pl.when(jnp.logical_not(self_solid))(far.wait_send)

    def wait_load(t):
        for q in range(n_grp):
            pltpu.make_async_copy(
                load_send.at[t], load_recv.at[t, q], recv_sem.at[t * n_msg + 11 + q]
            ).wait()

    n_floor = STEPS * n_msg

    def floor_copies(t, q):
        k = n_floor + t * n_grp
        src = V.at[2, 0, :, pl.ds(q * ow, ow)]
        far = pltpu.make_async_remote_copy(
            src_ref=src,
            dst_ref=floor_recv.at[t],
            send_sem=send_sem.at[k + q],
            recv_sem=recv_sem.at[k],
            device_id=owners[q],
            device_id_type=MESH,
        )
        near = pltpu.make_async_copy(src, floor_recv.at[t], recv_sem.at[k])
        return far, near

    def send_floor(t):
        for q in range(n_grp):
            far, near = floor_copies(t, q)
            pl.when(top & jnp.logical_not(self_owner[q]))(far.start)
            pl.when(self_owner[q])(near.start)

    def wait_floor_sent(t):
        for q in range(n_grp):
            far, _ = floor_copies(t, q)
            pl.when(top & jnp.logical_not(self_owner[q]))(far.wait_send)

    def wait_floor(t):
        pltpu.make_async_copy(load_send.at[t], floor_recv.at[t], recv_sem.at[n_floor + t * n_grp]).wait()

    def pack_stress(t):
        pack_rows(xs_send.at[t], S, 1, ALONG_X, nx - 1)
        ys_send[t] = pack_cols(S, 1, ALONG_Y, ny - 1)

    def pack_motion(t):
        pack_rows(xv_send.at[t], V, 0, range(3), 0)
        yv_send[t] = pack_cols(V, 0, range(3), 0)

    def pack_ocean(t):
        first_col = jnp.zeros((nx, ow), F32)
        last_col = jnp.zeros((nx, ow), F32)
        for k in range(oz):
            p = PR[k]
            opx_send[t, k : k + 1, :] = p[0:1, :]
            oux_send[t, k : k + 1, :] = FL[0, k, nx - 1 : nx, :] + ocean_step * p[nx - 1 : nx, :]
            first_col = jnp.where(ocol == k, shift(p, 0, k), first_col)
            last_col = jnp.where(ocol == k, shift(FL[1, k] + ocean_step * p, ow - 1, k), last_col)
        opy_send[t] = first_col
        ouy_send[t] = last_col

    def ocean_inner(t):
        has_x, has_y = xp.astype(F32), rp.astype(F32)
        below = jnp.zeros((nx, ow), F32)
        p = PR[0]
        for k in range(oz):
            up = PR[k + 1] if k + 1 < oz else None
            next_x = jnp.where(orow == nx - 1, opx_recv[t, k : k + 1, :], pltpu.roll(p, nx - 1, 0))
            next_y = jnp.where(ocol == ow - 1, shift(opy_recv[t], k, ow - 1), pltpu.roll(p, ow - 1, 1))
            flow_x = FL[0, k] - ocean_step * (next_x - p)
            flow_y = FL[1, k] - ocean_step * (next_y - p)
            FL[0, k] = flow_x
            FL[1, k] = flow_y
            above = up if up is not None else gravity_term * H[...]
            lift = FL[2, k] - vertical_step * (above - p)
            FL[2, k] = lift
            edge_x = has_x * (oux_recv[t, k : k + 1, :] - ocean_step * p[0:1, :])
            edge_y = has_y * (shift(ouy_recv[t], k, 0) - ocean_step * p)
            prev_x = jnp.where(orow == 0, edge_x, pltpu.roll(flow_x, 1, 0))
            prev_y = jnp.where(ocol == 0, edge_y, pltpu.roll(flow_y, 1, 1))
            spread = flow_x - prev_x + (flow_y - prev_y)
            PR[k] = p - ocean_step * spread - vertical_step * (lift - below)
            below = lift
            p = up
        H[...] = H[...] + surface_step * below

    def solid_velocity(t):
        unpack_cols(ys_recv[t], 0)
        S[XZ, 0] = zs_recv[t, 0]
        S[YZ, 0] = zs_recv[t, 1]

        @pl.when(zp)
        def _():
            S[ZZ, 0] = zs_recv[t, 2]

        @pl.when(top)
        def _():
            wait_load(t)
            weight = jnp.concatenate([load_recv[t, q] for q in range(n_grp)], axis=1)
            if t > 0:
                weight = weight + vertical_step * V[2, 0]
            S[ZZ, 0] = -weight

        @pl.loop(0, nz)
        def _(z):
            factor = BU[z]
            for k in range(3):
                along_x, along_y, along_z = (
                    S[ALONG_X[k], z + 1],
                    S[ALONG_Y[k], z + 1],
                    S[ALONG_Z[k], z + 1],
                )
                prev_x = jnp.where(row == 0, xs_recv[t, z, k : k + 1, :], pltpu.roll(along_x, 1, 0))
                prev_y = jnp.where(col == 0, widen(YH[k, z], False), pltpu.roll(along_y, 1, 1))
                prev_z = S[ALONG_Z[k], z]
                div = (along_x - prev_x) + (along_y - prev_y) + (along_z - prev_z)
                V[k, z] = V[k, z] + factor * div

    def solid_stress(t, write):
        unpack_cols(yv_recv[t], lanes - 1)
        for k in range(3):
            V[k, nz] = zv_recv[t, k]
        cohesion, friction = plastic[0], plastic[1]

        @pl.loop(0, nz)
        def _(z):
            grad = []
            for k in range(3):
                v = V[k, z]
                next_x = jnp.where(row == nx - 1, xv_recv[t, z, k : k + 1, :], pltpu.roll(v, nx - 1, 0))
                next_y = jnp.where(col == ny - 1, widen(YH[k, z], True), pltpu.roll(v, ny - 1, 1))
                next_z = V[k, z + 1]
                grad.append((next_x - v, next_y - v, next_z - v))
            lam, mu = LAM[z], MU[z]
            dil = lam * (grad[0][0] + grad[1][1] + grad[2][2])
            twice = 2.0 * mu
            sxx = S[XX, z + 1] + (dil + twice * grad[0][0])
            syy = S[YY, z + 1] + (dil + twice * grad[1][1])
            szz = S[ZZ, z + 1] + (dil + twice * grad[2][2])
            sxy = S[XY, z + 1] + mu * (grad[0][1] + grad[1][0])
            sxz = S[XZ, z + 1] + mu * (grad[0][2] + grad[2][0])
            syz = S[YZ, z + 1] + mu * (grad[1][2] + grad[2][1])
            mean = (sxx + syy + szz) * (1.0 / 3.0)
            dxx, dyy, dzz = sxx - mean, syy - mean, szz - mean
            tau = jnp.sqrt(0.5 * (dxx * dxx + dyy * dyy + dzz * dzz) + sxy * sxy + sxz * sxz + syz * syz)
            strength = cohesion + friction * jnp.maximum(-mean, 0.0)
            scale = jnp.where(FM[z] == 1, strength / jnp.maximum(tau, strength), 1.0)
            S[XX, z + 1] = mean + dxx * scale
            S[YY, z + 1] = mean + dyy * scale
            S[ZZ, z + 1] = mean + dzz * scale
            S[XY, z + 1] = sxy * scale
            S[XZ, z + 1] = sxz * scale
            S[YZ, z + 1] = syz * scale

    for k in range(3):
        loads[k].wait()
    pack_stress(0)
    pack_ocean(0)
    load_send[0] = PR[0]
    loads[3].wait()
    loads[4].wait()

    @pl.loop(0, nz)
    def _(z):
        ids = ID[z]
        fields = [jnp.zeros((nx, ny), F32)] * 3
        for region in range(REGIONS):
            here = ids == region
            fields = [jnp.where(here, mat[k, region], fields[k]) for k in range(3)]
        LAM[z] = courant_number * fields[0]
        MU[z] = courant_number * fields[1]
        BU[z] = courant_number * fields[2]

    for k in range(5, len(loads)):
        loads[k].wait()
    pl.semaphore_wait(barrier, expected)

    for t in range(STEPS):
        stress, motion, ocean = routes(t)
        last = t == STEPS - 1
        if t > 0:
            pack_stress(t)
        for message in stress:
            message.start()
        if t > 0:
            wait_floor(t - 1)
            PR[0] = PR[0] + vertical_step * floor_recv[t - 1]
            pack_ocean(t)
        for message in ocean:
            message.start()
        if t == 0:
            send_load(0)
        for message in ocean:
            message.wait_recv()
        ocean_inner(t)
        if not last:
            load_send[t + 1] = PR[0]
            send_load(t + 1)

        for message in stress:
            message.wait_recv()
        if t > 0:
            for message in before:
                message.wait_send()
            wait_floor_sent(t - 1)
        solid_velocity(t)
        pack_motion(t)
        for message in motion:
            message.start()
        send_floor(t)
        for message in stress:
            message.wait_send()
        for message in motion:
            message.wait_recv()
        solid_stress(t, last)
        for message in ocean:
            message.wait_send()
        wait_load_sent(t)
        before = motion

    outs = [
        pltpu.make_async_copy(source, target, out_sem.at[k])
        for k, (source, target) in enumerate(
            (
                (S.at[:, pl.ds(1, nz)], stress_out),
                (V.at[:, pl.ds(0, nz)], velocity_out),
                (FL, flow_out),
                (H, surface_out),
                (PR, pressure_out),
            )
        )
    ]
    for out in outs[:4]:
        out.start()
    wait_floor(STEPS - 1)
    PR[0] = PR[0] + vertical_step * floor_recv[STEPS - 1]
    outs[4].start()
    for message in before:
        message.wait_send()
    wait_floor_sent(STEPS - 1)
    for out in outs:
        out.wait()


def body(sizes, *arrays):
    n_grp = sizes[0]
    _, nz, nx, ny = arrays[0].shape
    oz, _, ow = arrays[2].shape
    lanes = min(128, ny)
    rows, cols, planes = (STEPS, nz, 4, ny), (STEPS, nx, lanes), (STEPS, 3, nx, ny)
    ocean_rows, ocean_cols = (STEPS, oz, ow), (STEPS, nx, ow)
    shapes = (
        [(6, nz + 1, nx, ny), (3, nz + 1, nx, ny), (oz, nx, ow), (3, oz, nx, ow), (nx, ow)]
        + [None] * 2
        + [(nz, nx, ny)] * 3
        + [rows] * 4
        + [cols] * 4
        + [planes] * 2
        + [(3, nz, nx, lanes)]
        + [ocean_rows] * 4
        + [ocean_cols] * 4
        + [(STEPS, nx, ow), (STEPS, n_grp, nx, ow), (STEPS, nx, ow)]
    )
    scratch = [
        pltpu.VMEM((nz, nx, ny), jnp.int32) if shape is None else pltpu.VMEM(shape, F32) for shape in shapes
    ]
    n_sem = STEPS * (15 + n_grp)
    scratch += [
        pltpu.SMEM(arrays[5].shape, F32),
        pltpu.SMEM(arrays[8].shape, F32),
        pltpu.SemaphoreType.DMA((9,)),
        pltpu.SemaphoreType.DMA((5,)),
        pltpu.SemaphoreType.DMA((n_sem,)),
        pltpu.SemaphoreType.DMA((n_sem,)),
    ]
    return pl.pallas_call(
        functools.partial(kernel, sizes),
        out_shape=[jax.ShapeDtypeStruct(arrays[k].shape, F32) for k in range(5)],
        in_specs=[pl.BlockSpec(memory_space=pl.ANY)] * 9,
        out_specs=[pl.BlockSpec(memory_space=pl.ANY)] * 5,
        scratch_shapes=scratch,
        compiler_params=pltpu.CompilerParams(collective_id=0, has_side_effects=True),
    )(*arrays)


def solution(mesh):
    sizes = (mesh.shape["grp"], mesh.shape["gx"], mesh.shape["gy"])
    solid, ocean = P(None, "grp", "gx", "gy"), P(None, "gx", ("grp", "gy"))
    flow, surface = P(None, None, "gx", ("grp", "gy")), P("gx", ("grp", "gy"))
    cells = P("grp", "gx", "gy")
    return jax.shard_map(
        functools.partial(body, sizes),
        mesh=mesh,
        in_specs=(solid, solid, ocean, flow, surface, P(), cells, cells, P()),
        out_specs=(solid, solid, ocean, flow, surface),
        check_vma=False,
    )
```

```python
import functools

import jax
import jax.numpy as jnp
from jax import lax
from jax.experimental import pallas as pl
from jax.experimental.pallas import tpu as pltpu
from jax.sharding import PartitionSpec as P

STEPS = 2
REGIONS = 8

courant_number = 0.2
ocean_step = 0.3
vertical_step = 0.3
gravity_term = 0.5
surface_step = 0.3

MESH = pl.DeviceIdType.MESH
F32 = jnp.float32
XX, YY, ZZ, XY, XZ, YZ = range(6)
ALONG_X = (XX, XY, XZ)
ALONG_Y = (XY, YY, YZ)
ALONG_Z = (XZ, YZ, ZZ)
EDGE = 8


class Route:
    def __init__(self, src, dst, send_sem, recv_sem, device, sends, receives, here=None):
        self.copy = pltpu.make_async_remote_copy(
            src_ref=src,
            dst_ref=dst,
            send_sem=send_sem,
            recv_sem=recv_sem,
            device_id=device,
            device_id_type=MESH,
        )
        self.sends, self.receives, self.here = sends, receives, here
        if here is not None:
            self.local = pltpu.make_async_copy(src, dst, recv_sem)

    def start(self):
        pl.when(self.sends)(self.copy.start)
        if self.here is not None:
            pl.when(self.here)(self.local.start)

    def wait_recv(self):
        pl.when(self.receives)(self.copy.wait_recv)

    def wait_send(self):
        pl.when(self.sends)(self.copy.wait_send)


BUFFERS = (
    "xs_send", "xs_recv", "xw_send", "xw_recv", "ys_send", "ys_recv",
    "yw_send", "yw_recv", "by_send", "by_recv", "zs_recv", "zw_recv",
    "bz_recv", "ezx_send", "ezx_recv", "ezy_send", "ezy_recv", "exy_send",
    "exy_recv", "eyx_recv", "exz_recv", "eyz_recv", "opx_send", "opx_recv",
    "oux_send", "oux_recv", "opy_send", "opy_recv", "ouy_send", "ouy_recv",
    "load_send", "row_send", "col_send", "fw_recv", "fb_recv", "fx_recv",
    "fy_recv",
)


def buffer_shapes(nz, nx, ny, oz, ow):
    two = STEPS
    rows, cols = (two, nz, 4, ny), (two, nx, ow)
    shapes = {name: cols for name in BUFFERS}
    for name in ("xs_send", "xs_recv", "xw_send", "xw_recv"):
        shapes[name] = rows
    for name in ("zs_recv", "zw_recv"):
        shapes[name] = (two, 3, nx, ny)
    for name in ("ezx_send", "ezx_recv", "exz_recv"):
        shapes[name] = (two, 4, ny)
    for name in ("exy_recv", "eyx_recv"):
        shapes[name] = (two, EDGE, ow)
    for name in ("row_send", "fx_recv"):
        shapes[name] = (two, 4, ow)
    for name in ("opx_send", "opx_recv", "oux_send", "oux_recv"):
        shapes[name] = (two, oz, ow)
    for name in ("by_send", "by_recv", "fb_recv"):
        shapes[name] = (nx, ow)
    shapes["bz_recv"] = (nx, ny)
    return [shapes[name] for name in BUFFERS]


def kernel(sizes, *refs):
    velocity_in, stress_in, pressure_in, flow_in, surface_in, materials_in, regions_in, fault_in, plastic_in = refs[:9]
    S, V, PR, FL, H = refs[9:14]
    ID, FM, LAM, MU, BU, YH = refs[14:20]
    buf = dict(zip(BUFFERS, refs[20 : 20 + len(BUFFERS)]))
    mat, plastic, in_sem, send_sem, recv_sem = refs[20 + len(BUFFERS) :]

    n_grp, n_gx, n_gy = sizes
    nz, nx, ny = ID.shape
    oz, _, ow = PR.shape
    lanes = ow
    g, a, b = lax.axis_index("grp"), lax.axis_index("gx"), lax.axis_index("gy")

    loads = [
        pltpu.make_async_copy(source, target, in_sem.at[k])
        for k, (source, target) in enumerate(
            (
                (stress_in, S.at[:, pl.ds(1, nz)]),
                (pressure_in, PR),
                (flow_in, FL),
                (materials_in, mat),
                (regions_in, ID),
                (velocity_in, V.at[:, pl.ds(0, nz)]),
                (surface_in, H),
                (fault_in, FM),
                (plastic_in, plastic),
            )
        )
    ]
    for load in loads:
        load.start()

    rank = g * n_gy + b
    n_rank = n_grp * n_gy
    no = jnp.logical_not
    xp, xn = a > 0, a < n_gx - 1
    yp, yn = b > 0, b < n_gy - 1
    zp, zn = g > 0, g < n_grp - 1
    rp, rn = rank > 0, rank < n_rank - 1
    top = no(zp)

    def at(dg, da, db):
        return (
            jnp.clip(g + dg, 0, n_grp - 1),
            jnp.clip(a + da, 0, n_gx - 1),
            jnp.clip(b + db, 0, n_gy - 1),
        )

    def of_rank(r, da=0):
        return (r // n_gy, jnp.clip(a + da, 0, n_gx - 1), r % n_gy)

    dev_rp = of_rank(jnp.maximum(rank - 1, 0))
    dev_rn = of_rank(jnp.minimum(rank + 1, n_rank - 1))
    solid = rank // n_grp
    quarter = rank % n_grp
    leads = quarter == 0
    dev_solid = (0, a, solid)
    self_solid = top & (solid == b)
    owners = [of_rank(b * n_grp + q) for q in range(n_grp)]
    self_owner = [top & (b * n_grp + q == b) for q in range(n_grp)]
    after = jnp.minimum(b + 1, n_gy - 1) * n_grp

    barrier = pltpu.get_barrier_semaphore()
    both = [
        (xp, at(0, -1, 0)),
        (xn, at(0, 1, 0)),
        (xp & yn, at(0, -1, 1)),
        (xn & yp, at(0, 1, -1)),
        (xp & zn, at(1, -1, 0)),
        (xn & zp, at(-1, 1, 0)),
        (yn & zp, at(-1, 0, 1)),
        (yp & zn, at(1, 0, -1)),
        (zp, at(-1, 0, 0)),
        (zn, at(1, 0, 0)),
        (yp, at(0, 0, -1)),
        (yn, at(0, 0, 1)),
        (rp, dev_rp),
        (rn, dev_rn),
        (no(self_solid), dev_solid),
    ] + [(top & no(self_owner[q]), owners[q]) for q in range(n_grp)]
    both += [(top & xn, of_rank(b * n_grp + q, 1)) for q in range(n_grp)]
    both += [(xp, (0, jnp.maximum(a - 1, 0), solid))]
    both += [(top & yn, of_rank(after))]
    both += [(leads & (solid > 0), (0, a, jnp.maximum(solid - 1, 0)))]
    expected = 0
    for there, device in both:
        expected = expected + there.astype(jnp.int32)

        @pl.when(there)
        def _(device=device):
            pl.semaphore_signal(barrier, inc=1, device_id=device, device_id_type=MESH)

    for missing, names in (
        (no(xp), ("xs_recv", "oux_recv",)),
        (no(xn), ("xw_recv", "opx_recv", "ezx_recv", "eyx_recv",)),
        (no(yp), ("ys_recv",)),
        (no(yn), ("yw_recv", "by_recv", "ezy_recv", "exy_recv",)),
        (top, ("zs_recv",)),
        (no(zn), ("zw_recv", "bz_recv", "exz_recv", "eyz_recv",)),
        (no(rp), ("ouy_recv",)),
        (no(rn), ("opy_recv",)),
        (xn & no(yp), ("eyx_recv",)),
        (yn & no(xp), ("exy_recv",)),
        (zn & no(xp), ("exz_recv",)),
        (zn & no(yp), ("eyz_recv",)),
        (no(xp), ("fx_recv",)),
        (no(leads & (solid > 0)), ("fy_recv",)),
    ):

        @pl.when(missing)
        def _(names=names):
            for name in names:
                area = buf[name].at[:, pl.ds(0, 2)] if name == "zs_recv" else buf[name]
                area[...] = jnp.zeros(area.shape, F32)

    lane = lax.broadcasted_iota(jnp.int32, (nx, lanes), 1)
    line = lax.broadcasted_iota(jnp.int32, (nx, lanes), 0)
    row = lax.broadcasted_iota(jnp.int32, (nx, ny), 0)
    col = lax.broadcasted_iota(jnp.int32, (nx, ny), 1)
    first_lane = lax.broadcasted_iota(jnp.int32, (1, lanes), 1) == 0

    def shift(tile, start, stop):
        amount = (stop - start) % tile.shape[1]
        return pltpu.roll(tile, amount, 1) if amount else tile

    def pack_cols(field, planes, comps, where, zs):
        first = (where // lanes) * lanes
        packed = jnp.zeros((nx, lanes), F32)
        for z in zs:
            for k, c in enumerate(comps):
                tile = field[c, z + planes, :, first : first + lanes]
                slot = (z - zs[0]) * 3 + k
                packed = jnp.where(lane == slot, shift(tile, where - first, slot), packed)
        return packed

    def widen(tile, last):
        if ny == lanes:
            return tile
        blank = jnp.zeros((tile.shape[0], ny - lanes), F32)
        return jnp.concatenate([blank, tile] if last else [tile, blank], axis=1)

    counter = [0]

    def route(src, dst, device, sends, receives):
        k = counter[0]
        counter[0] += 1
        return Route(src, dst, send_sem.at[k], recv_sem.at[k], device, sends, receives)

    def twin(name, t):
        return buf[name + "_send"].at[t], buf[name + "_recv"].at[t]

    steps = []
    for t in range(STEPS):
        plan = {}
        xs, ys = buf["xs_send"].at[t], buf["ys_send"].at[t]
        plan["stress"] = [
            route(xs, buf["xs_recv"].at[t], at(0, 1, 0), xn, xp),
            route(*twin("ezx", t), at(1, -1, 0), xp & zn, xn & zp),
            route(xs.at[0], buf["exz_recv"].at[t], at(-1, 1, 0), xn & zp, xp & zn),
            route(ys.at[pl.ds(0, EDGE)], buf["eyx_recv"].at[t], at(0, -1, 1), xp & yn, xn & yp),
            route(
                buf["exy_send"].at[t, pl.ds(nx - EDGE, EDGE)],
                buf["exy_recv"].at[t],
                at(0, 1, -1),
                xn & yp,
                xp & yn,
            ),
            route(S.at[pl.ds(XZ, 2), nz], buf["zs_recv"].at[t, pl.ds(0, 2)], at(1, 0, 0), zn, zp),
            route(S.at[ZZ, nz], buf["zs_recv"].at[t, 2], at(1, 0, 0), zn, zp),
            route(ys, buf["ys_recv"].at[t], at(0, 0, 1), yn, yp),
            route(ys, buf["eyz_recv"].at[t], at(-1, 0, 1), yn & zp, yp & zn),
            route(*twin("ezy", t), at(1, 0, -1), yp & zn, yn & zp),
        ]
        if t == 0:
            plan["once"] = [
                route(BU.at[0], buf["bz_recv"], at(-1, 0, 0), zp, zn),
                route(buf["by_send"], buf["by_recv"], at(0, 0, -1), yp, yn),
            ]
        base = counter[0]
        plan["beside"] = []
        for q in range(n_grp):
            plan["beside"].append(
                Route(
                    xs.at[0, :, pl.ds(q * ow, ow)],
                    buf["fx_recv"].at[t],
                    send_sem.at[base + q],
                    recv_sem.at[base],
                    of_rank(b * n_grp + q, 1),
                    top & xn,
                    xp,
                )
            )
        counter[0] += n_grp
        plan["beside"].append(route(ys, buf["fy_recv"].at[t], of_rank(after), top & yn, leads & (solid > 0)))
        plan["motion"] = [
            route(*twin("xw", t), at(0, -1, 0), xp, xn),
            route(V.at[:, 0], buf["zw_recv"].at[t], at(-1, 0, 0), zp, zn),
            route(*twin("yw", t), at(0, 0, -1), yp, yn),
        ]
        plan["floor"] = []
        sources = [(V.at[2, 0], buf["fw_recv"].at[t])] + ([(BU.at[0], buf["fb_recv"])] if t == 0 else [])
        for source, target in sources:
            for q in range(n_grp):
                plan["floor"].append(
                    Route(
                        source.at[:, pl.ds(q * ow, ow)],
                        target,
                        send_sem.at[counter[0] + q],
                        recv_sem.at[counter[0]],
                        owners[q],
                        top & no(self_owner[q]),
                        True,
                        self_owner[q],
                    )
                )
            counter[0] += n_grp
        plan["ocean"] = [
            route(*twin("opx", t), at(0, -1, 0), xp, xn),
            route(*twin("oux", t), at(0, 1, 0), xn, xp),
            route(*twin("opy", t), dev_rp, rp, rn),
            route(*twin("ouy", t), dev_rn, rn, rp),
        ]
        base = counter[0]
        spot = pl.ds(pl.multiple_of(quarter * ow, ow), ow)
        plan["load"] = [
            Route(
                buf["load_send"].at[t],
                buf["zs_recv"].at[t, 2, :, spot],
                send_sem.at[base],
                recv_sem.at[base + quarter],
                dev_solid,
                no(self_solid),
                None,
                self_solid,
            ),
            Route(
                buf["row_send"].at[t],
                buf["ezx_recv"].at[t, :, spot],
                send_sem.at[base + 1],
                recv_sem.at[base + n_grp + quarter],
                (0, jnp.maximum(a - 1, 0), solid),
                xp,
                None,
            ),
            Route(
                buf["col_send"].at[t],
                buf["ezy_recv"].at[t],
                send_sem.at[base + 2],
                recv_sem.at[base + 2 * n_grp],
                (0, a, jnp.maximum(solid - 1, 0)),
                leads & (solid > 0),
                top & yn,
            ),
        ]
        plan["loaded"] = [plan["load"][2]]
        for q in range(n_grp):
            place = pl.ds(q * ow, ow)
            for k, area, there in (
                (q, buf["zs_recv"].at[t, 2, :, place], top),
                (n_grp + q, buf["ezx_recv"].at[t, :, place], top & xn),
            ):
                plan["loaded"].append(
                    Route(area, area, send_sem.at[base], recv_sem.at[base + k], dev_solid, there, there)
                )
        counter[0] += 2 * n_grp + 3
        steps.append(plan)

    def start(*groups):
        for group in groups:
            for message in group:
                message.start()

    def arrive(*groups):
        for group in groups:
            for message in group:
                message.wait_recv()

    def leave(*groups):
        for group in groups:
            for message in group:
                message.wait_send()

    def pack_stress(t):
        for z in range(nz):
            for k, c in enumerate(ALONG_X):
                buf["xs_send"][t, z, k : k + 1, :] = S[c, z + 1, nx - 1 : nx, :]
        for k, c in enumerate(ALONG_Z):
            buf["ezx_send"][t, k : k + 1, :] = S[c, nz, 0:1, :]
        buf["exy_send"][t] = pack_cols(S, 1, ALONG_X, 0, range(nz))
        buf["ys_send"][t] = pack_cols(S, 1, ALONG_Y, ny - 1, range(nz))
        buf["ezy_send"][t] = pack_cols(S, 1, ALONG_Z, 0, range(nz - 1, nz))

    def pack_motion(t):
        for z in range(nz):
            for k in range(3):
                buf["xw_send"][t, z, k : k + 1, :] = V[k, z, 0:1, :]
            buf["xw_send"][t, z, 3:4, :] = BU[z, 0:1, :]
        buf["yw_send"][t] = pack_cols(V, 0, range(3), 0, range(nz))

    def set_load(t):
        load = -PR[0]
        buf["load_send"][t] = load
        buf["row_send"][t] = jnp.zeros((4, ow), F32)
        buf["row_send"][t, 2:3, :] = load[0:1, :]
        buf["col_send"][t] = jnp.where(lane == 2, shift(load, 0, 2), 0.0)

    def pack_ocean(t):
        first_col = jnp.zeros((nx, ow), F32)
        last_col = jnp.zeros((nx, ow), F32)
        for k in range(oz):
            p = PR[k]
            buf["opx_send"][t, k : k + 1, :] = p[0:1, :]
            buf["oux_send"][t, k : k + 1, :] = FL[0, k, nx - 1 : nx, :] + ocean_step * p[nx - 1 : nx, :]
            first_col = jnp.where(lane == k, shift(p, 0, k), first_col)
            last_col = jnp.where(lane == k, shift(FL[1, k] + ocean_step * p, ow - 1, k), last_col)
        buf["opy_send"][t] = first_col
        buf["ouy_send"][t] = last_col

    def ocean_inner(t):
        has_x, has_y = xp.astype(F32), rp.astype(F32)
        below = jnp.zeros((nx, ow), F32)
        p = PR[0]
        for k in range(oz):
            up = PR[k + 1] if k + 1 < oz else None
            next_x = jnp.where(line == nx - 1, buf["opx_recv"][t, k : k + 1, :], pltpu.roll(p, nx - 1, 0))
            next_y = jnp.where(lane == ow - 1, shift(buf["opy_recv"][t], k, ow - 1), pltpu.roll(p, ow - 1, 1))
            flow_x = FL[0, k] - ocean_step * (next_x - p)
            flow_y = FL[1, k] - ocean_step * (next_y - p)
            FL[0, k] = flow_x
            FL[1, k] = flow_y
            above = up if up is not None else gravity_term * H[...]
            lift = FL[2, k] - vertical_step * (above - p)
            FL[2, k] = lift
            edge_x = has_x * (buf["oux_recv"][t, k : k + 1, :] - ocean_step * p[0:1, :])
            edge_y = has_y * (shift(buf["ouy_recv"][t], k, 0) - ocean_step * p)
            prev_x = jnp.where(line == 0, edge_x, pltpu.roll(flow_x, 1, 0))
            prev_y = jnp.where(lane == 0, edge_y, pltpu.roll(flow_y, 1, 1))
            spread = flow_x - prev_x + (flow_y - prev_y)
            PR[k] = p - ocean_step * spread - vertical_step * (lift - below)
            below = lift
            p = up
        H[...] = H[...] + surface_step * below

    def ocean_floor(t):
        beside = buf["load_send"][t]
        beside = beside + jnp.where(line == 0, buf["fx_recv"][t, 2:3, :], 0.0)
        beside = beside + jnp.where(lane == 0, shift(buf["fy_recv"][t], 2, 0), 0.0)
        PR[0] = PR[0] + vertical_step * (buf["fw_recv"][t] - buf["fb_recv"][...] * beside)

    def partial_velocity():
        @pl.loop(0, nz)
        def _(z):
            factor = BU[z]
            for k in range(3):
                along_x, along_y, along_z = (
                    S[ALONG_X[k], z + 1],
                    S[ALONG_Y[k], z + 1],
                    S[ALONG_Z[k], z + 1],
                )
                prev_x = jnp.where(row == 0, 0.0, pltpu.roll(along_x, 1, 0))
                prev_y = jnp.where(col == 0, 0.0, pltpu.roll(along_y, 1, 1))
                prev_z = S[ALONG_Z[k], z]
                div = (along_x - prev_x) + (along_y - prev_y) + (along_z - prev_z)
                V[k, z] = V[k, z] + factor * div

    def complete_velocity(t):
        head = slice(0, lanes)
        extra = jnp.where(line == 0, buf["exy_recv"][t, EDGE - 1 : EDGE, :], 0.0)
        extra = extra + jnp.where(lane < 3, buf["ezy_recv"][t], 0.0)
        ahead = buf["yw_recv"][t] - buf["by_recv"][...] * (buf["ys_send"][t] + extra)
        ys, eyx, eyz = buf["ys_recv"][t], buf["eyx_recv"][t], buf["eyz_recv"][t]
        for z in range(nz):
            weight = BU[z, :, head]
            for k in range(3):
                slot = z * 3 + k
                YH[k, z] = shift(ahead, slot, lanes - 1)
                V[k, z, :, head] = V[k, z, :, head] - jnp.where(lane == 0, weight * shift(ys, slot, 0), 0.0)
                V[k, z, 0:1, :] = V[k, z, 0:1, :] - BU[z, 0:1, :] * buf["xs_recv"][t, z, k : k + 1, :]
                beside = buf["xs_send"][t, z, k : k + 1, :]
                beside = beside + widen(jnp.where(first_lane, shift(eyx, slot, 0)[0:1, :], 0.0), False)
                if z == 0:
                    beside = beside + buf["ezx_recv"][t, k : k + 1, :]
                buf["xw_recv"][t, z, k : k + 1, :] = (
                    buf["xw_recv"][t, z, k : k + 1, :] - buf["xw_recv"][t, z, 3:4, :] * beside
                )
        for k in range(3):
            V[k, 0] = V[k, 0] - BU[0] * buf["zs_recv"][t, k]
            beside = S[ALONG_Z[k], nz] + jnp.where(row == 0, buf["exz_recv"][t, k : k + 1, :], 0.0)
            beside = beside + widen(jnp.where(lane == 0, shift(eyz, k, 0), 0.0), False)
            V[k, nz] = buf["zw_recv"][t, k] - buf["bz_recv"][...] * beside

    def solid_stress(t):
        cohesion, friction = plastic[0], plastic[1]

        @pl.loop(0, nz)
        def _(z):
            grad = []
            for k in range(3):
                v = V[k, z]
                next_x = jnp.where(row == nx - 1, buf["xw_recv"][t, z, k : k + 1, :], pltpu.roll(v, nx - 1, 0))
                next_y = jnp.where(col == ny - 1, widen(YH[k, z], True), pltpu.roll(v, ny - 1, 1))
                next_z = V[k, z + 1]
                grad.append((next_x - v, next_y - v, next_z - v))
            lam, mu = LAM[z], MU[z]
            dil = lam * (grad[0][0] + grad[1][1] + grad[2][2])
            twice = 2.0 * mu
            sxx = S[XX, z + 1] + (dil + twice * grad[0][0])
            syy = S[YY, z + 1] + (dil + twice * grad[1][1])
            szz = S[ZZ, z + 1] + (dil + twice * grad[2][2])
            sxy = S[XY, z + 1] + mu * (grad[0][1] + grad[1][0])
            sxz = S[XZ, z + 1] + mu * (grad[0][2] + grad[2][0])
            syz = S[YZ, z + 1] + mu * (grad[1][2] + grad[2][1])
            mean = (sxx + syy + szz) * (1.0 / 3.0)
            dxx, dyy, dzz = sxx - mean, syy - mean, szz - mean
            tau = jnp.sqrt(0.5 * (dxx * dxx + dyy * dyy + dzz * dzz) + sxy * sxy + sxz * sxz + syz * syz)
            strength = cohesion + friction * jnp.maximum(-mean, 0.0)
            scale = jnp.where(FM[z] == 1, strength / jnp.maximum(tau, strength), 1.0)
            S[XX, z + 1] = mean + dxx * scale
            S[YY, z + 1] = mean + dyy * scale
            S[ZZ, z + 1] = mean + dzz * scale
            S[XY, z + 1] = sxy * scale
            S[XZ, z + 1] = sxz * scale
            S[YZ, z + 1] = syz * scale

    for c in ALONG_Z:
        S[c, 0] = jnp.zeros((nx, ny), F32)
    for k in range(3):
        loads[k].wait()
    pack_stress(0)
    pack_ocean(0)
    set_load(0)
    loads[3].wait()
    loads[4].wait()

    @pl.loop(0, nz)
    def _(z):
        ids = ID[z]
        fields = [jnp.zeros((nx, ny), F32)] * 3
        for region in range(REGIONS):
            here = ids == region
            fields = [jnp.where(here, mat[k, region], fields[k]) for k in range(3)]
        LAM[z] = courant_number * fields[0]
        MU[z] = courant_number * fields[1]
        BU[z] = courant_number * fields[2]

    packed = jnp.zeros((nx, lanes), F32)
    for z in range(nz):
        tile = BU[z, :, 0:lanes]
        for k in range(3):
            packed = jnp.where(lane == z * 3 + k, shift(tile, 0, z * 3 + k), packed)
    buf["by_send"][...] = packed
    for k in range(5, len(loads)):
        loads[k].wait()
    partial_velocity()
    pack_motion(0)
    pl.semaphore_wait(barrier, expected)

    for t, plan in enumerate(steps):
        last = t == STEPS - 1
        if t > 0:
            pack_stress(t)
            start(plan["stress"], plan["beside"])
            S[ZZ, 0] = (-vertical_step * top.astype(F32)) * V[2, 0]
            partial_velocity()
            pack_motion(t)
            start(plan["motion"], plan["floor"])
        else:
            start(plan["stress"][:5], plan["motion"], plan["stress"][5:])
            start(plan["load"], plan["ocean"], plan["once"], plan["floor"], plan["beside"])

        arrive(plan["ocean"])
        ocean_inner(t)
        if not last:
            set_load(t + 1)
            start(steps[t + 1]["load"])
        arrive(plan["beside"][-1:], plan["beside"][:1], plan["floor"][::n_grp])
        ocean_floor(t)
        if not last:
            pack_ocean(t + 1)
            start(steps[t + 1]["ocean"])

        leave(plan["motion"], plan["floor"])
        arrive(plan["stress"], plan["motion"], plan["loaded"])
        if t == 0:
            arrive(plan["once"])
        complete_velocity(t)
        leave(plan["stress"])
        solid_stress(t)

    for t, plan in enumerate(steps):
        leave(plan["beside"], plan["ocean"], plan["load"])
    leave(steps[0]["once"])


def n_semaphores(n_grp):
    return STEPS * (10 + n_grp + 1 + 3 + 2 * n_grp + 4 + 2 * n_grp + 3) + 2


def writer(S, V, PR, FL, H, velocity_out, stress_out, pressure_out, flow_out, surface_out, sem):
    nz = velocity_out.shape[1]
    copies = [
        pltpu.make_async_copy(source, target, sem.at[k])
        for k, (source, target) in enumerate(
            (
                (S.at[:, pl.ds(1, nz)], stress_out),
                (V.at[:, pl.ds(0, nz)], velocity_out),
                (FL, flow_out),
                (PR, pressure_out),
                (H, surface_out),
            )
        )
    ]
    for copy in copies:
        copy.start()
    for copy in copies:
        copy.wait()


def body(sizes, *arrays):
    n_grp = sizes[0]
    _, nz, nx, ny = arrays[0].shape
    oz, _, ow = arrays[2].shape
    n_sem = n_semaphores(n_grp)
    scratch = [pltpu.VMEM((nz, nx, ny), jnp.int32)] * 2 + [pltpu.VMEM((nz, nx, ny), F32)] * 3
    scratch += [pltpu.VMEM((3, nz, nx, ow), F32)]
    scratch += [pltpu.VMEM(shape, F32) for shape in buffer_shapes(nz, nx, ny, oz, ow)]
    scratch += [
        pltpu.SMEM(arrays[5].shape, F32),
        pltpu.SMEM(arrays[8].shape, F32),
        pltpu.SemaphoreType.DMA((9,)),
        pltpu.SemaphoreType.DMA((n_sem,)),
        pltpu.SemaphoreType.DMA((n_sem,)),
    ]
    states = [(6, nz + 1, nx, ny), (3, nz + 1, nx, ny)] + [arrays[k].shape for k in (2, 3, 4)]
    everywhere, resident = pl.BlockSpec(memory_space=pl.ANY), pl.BlockSpec(memory_space=pltpu.VMEM)
    state = pl.pallas_call(
        functools.partial(kernel, sizes),
        out_shape=[pltpu.VMEM(shape, F32) for shape in states],
        in_specs=[everywhere] * 9,
        out_specs=[resident] * 5,
        scratch_shapes=scratch,
        compiler_params=pltpu.CompilerParams(collective_id=0, has_side_effects=True),
        name="steps",
    )(*arrays)
    return pl.pallas_call(
        writer,
        out_shape=[jax.ShapeDtypeStruct(arrays[k].shape, F32) for k in range(5)],
        in_specs=[everywhere] * 5,
        out_specs=[everywhere] * 5,
        scratch_shapes=[pltpu.SemaphoreType.DMA((5,))],
        compiler_params=pltpu.CompilerParams(vmem_limit_bytes=1 << 20),
        name="write",
    )(*state)


def solution(mesh):
    sizes = (mesh.shape["grp"], mesh.shape["gx"], mesh.shape["gy"])
    solid, ocean = P(None, "grp", "gx", "gy"), P(None, "gx", ("grp", "gy"))
    flow, surface = P(None, None, "gx", ("grp", "gy")), P("gx", ("grp", "gy"))
    cells = P("grp", "gx", "gy")
    return jax.shard_map(
        functools.partial(body, sizes),
        mesh=mesh,
        in_specs=(solid, solid, ocean, flow, surface, P(), cells, cells, P()),
        out_specs=(solid, solid, ocean, flow, surface),
        check_vma=False,
    )
```
